32 devices in a mesh: rep: 2 (over y), row: 4 (over x, core), col: 4 (over z).
Axes of the slice: x: 2, y: 2, z: 4, core: 2. Of those that a mesh axis runs over, the one named last changes fastest.
Arguments:
- noise: bfloat16 [16, 4, 4, 1536], P('rep', 'row', 'col'), parts along dimension 0, may hold values from -6 to 6
- block_values: bfloat16 [8, 4, 8, 384, 384], P(('rep', 'row'), 'col'), parts along dimension 0, as said below
- block_rows: int32 [8, 4, 8], P(('rep', 'row'), 'col'), parts along dimension 0, may hold values from 0 to 15
- block_cols: int32 [8, 4, 8], P(('rep', 'row'), 'col'), parts along dimension 0, may hold values from 0 to 15
- block_count: int32 [8, 4], P(('rep', 'row'), 'col'), parts along dimension 0, may hold values from 2 to 8, as said below
- self_mobility: float32 [8, 6144], P(('rep', 'row')), parts along dimension 0, may hold values from 0.4 to 1.6
Outputs:
- first_term: bfloat16 [16, 4, 4, 1536], P('rep', 'col', 'row'), parts along dimension 0
- second_term: bfloat16 [16, 4, 4, 1536], P('rep', 'row', 'col'), parts along dimension 0
The draws below stay inside these ranges and needn't reach their ends.
There are 2 independent parts, one for each index of `rep`. The reference program is written for one: setup_inputs(seed, part) draws one part's arguments, and reference() takes and returns one part's arrays. A program takes and returns all parts, laid end to end along the dimension named above; each array names one. Nothing has to cross between parts.
Inputs may be any that keep to these rules, and one draw needn't show every extreme that they name: block_values, block_rows and block_cols describe a symmetric M: the slot list of owner (i, j) is that of owner (j, i) with rows and columns swapped and blocks transposed, slot by slot; on owners with i = j, slots 2k and 2k + 1 hold a block and its transpose with swapped rows and columns. `block_count`: even, equal on owners (i, j) and (j, i); owners with |i - j| <= 1 have exactly 8 live slots; owners (0, 3) and (3, 0) have exactly 2.
All inputs are finite; a program needn't handle non-finite values.
Results may differ from the reference program's by a relative error of at most 0.014.
Values may be sent and summed in bfloat16 or wider, within the bound.
No kernel may reach another device: no remote copies, remote signals or barrier semaphores. Data moves between devices by JAX's collectives and lax.ppermute only.
A program may use at most 64 MiB of HBM per device.

```python
import math
import jax
import jax.numpy as jnp
from jax import lax

CB = 128
NVEC = 8
SLOTS = 8
GB = 16
GROUP_LEN = 6144
PIECE = 1536
N_ROW = 4
N_COL = 4


def slot_layout(key):
    device_total = N_ROW * N_COL
    device_ids = jnp.arange(device_total, dtype=jnp.int32)
    owner_row = device_ids // N_COL
    owner_col = device_ids % N_COL
    lower_owner = jnp.minimum(owner_row, owner_col)
    upper_owner = jnp.maximum(owner_row, owner_col)
    canonical = lower_owner * N_COL + upper_owner
    slot_ids = jnp.arange(SLOTS, dtype=jnp.int32)
    base_rows = jax.random.randint(jax.random.fold_in(key, 11), (device_total, SLOTS), 0, GB, dtype=jnp.int32)
    base_cols = jax.random.randint(jax.random.fold_in(key, 12), (device_total, SLOTS), 0, GB, dtype=jnp.int32)
    half_count = jax.random.randint(jax.random.fold_in(key, 13), (device_total,), 1, SLOTS // 2 + 1, dtype=jnp.int32)
    half_count = jnp.where(device_ids == N_COL - 1, 1, half_count).astype(jnp.int32)
    on_diagonal = owner_row == owner_col
    source_slot = jnp.where(on_diagonal[:, None], slot_ids[None, :] - slot_ids[None, :] % 2, slot_ids[None, :])
    swapped = jnp.where(on_diagonal[:, None], slot_ids[None, :] % 2 == 1, (owner_row > owner_col)[:, None])
    first_rows = jnp.take_along_axis(base_rows[canonical], source_slot, axis=1)
    first_cols = jnp.take_along_axis(base_cols[canonical], source_slot, axis=1)
    rows_out = jnp.where(swapped, first_cols, first_rows)
    cols_out = jnp.where(swapped, first_rows, first_cols)
    near_band = jnp.abs(owner_row - owner_col) <= 1
    counts_out = jnp.where(near_band, SLOTS, 2 * half_count[canonical]).astype(jnp.int32)
    return (rows_out, cols_out, counts_out, canonical, source_slot, swapped)


def draw_block_rows(key, part):
    rows_out = slot_layout(key)[0]
    return rows_out.reshape(N_ROW, N_COL, SLOTS)


def draw_block_cols(key, part):
    cols_out = slot_layout(key)[1]
    return cols_out.reshape(N_ROW, N_COL, SLOTS)


def draw_block_count(key, part):
    counts_out = slot_layout(key)[2]
    return counts_out.reshape(N_ROW, N_COL)


def draw_block_values(key, part):
    layout = slot_layout(key)
    canonical = layout[3]
    source_slot = layout[4]
    swapped = layout[5]
    span_len = 3 * CB
    spread_scale = 0.3 / math.sqrt(span_len * SLOTS)
    value_key = jax.random.fold_in(key, 21)

    def one_device(dev_id):

        def one_slot(slot_id):
            sub_key = jax.random.fold_in(value_key, canonical[dev_id] * SLOTS + source_slot[dev_id, slot_id])
            tile_vals = jax.random.normal(sub_key, (span_len, span_len), jnp.float32)
            tile_vals = jnp.where(swapped[dev_id, slot_id], tile_vals.T, tile_vals)
            return (spread_scale * tile_vals).astype(jnp.bfloat16)
        return lax.map(one_slot, jnp.arange(SLOTS, dtype=jnp.int32))
    values_out = lax.map(one_device, jnp.arange(N_ROW * N_COL, dtype=jnp.int32))
    return values_out.reshape(N_ROW, N_COL, SLOTS, span_len, span_len)


def block_scale(key, shape, pieces, low, largest):
    def one(dim, blocks):
        steps = jax.random.uniform(jax.random.fold_in(jax.random.fold_in(key, 6), dim), (blocks,), jnp.float32, low / len(pieces), largest / len(pieces))
        return jnp.repeat(jnp.exp(steps), shape[dim] // blocks).reshape((-1,) + (1,) * (len(shape) - dim - 1))

    gain = one(*pieces[0])
    for cut in pieces[1:]:
        gain = gain * one(*cut)
    return gain


def centred(stream_key, shape, spread, reach, split=(), kind=jnp.bfloat16):
    entries = spread * jax.random.normal(stream_key, shape, jnp.float32)
    if split:
        entries = entries * block_scale(stream_key, shape, split, -0.22, 0.18)
    return jnp.clip(entries, -reach, reach).astype(kind)


def setup_inputs(seed: int = 0, part: int = 0) -> dict:
    keys = jax.random.split(jax.random.key(seed), 7)
    own_keys = jax.random.split(jax.random.fold_in(keys[6], part), 7)
    return {
        "noise": centred(own_keys[0], (NVEC, N_ROW, N_COL, PIECE), 1.0, 6.0, ((1, 4), (2, 4))),
        "block_values": draw_block_values(jax.random.fold_in(jax.random.fold_in(keys[6], part), 71), part),
        "block_rows": draw_block_rows(jax.random.fold_in(jax.random.fold_in(keys[6], part), 71), part),
        "block_cols": draw_block_cols(jax.random.fold_in(jax.random.fold_in(keys[6], part), 71), part),
        "block_count": draw_block_count(jax.random.fold_in(jax.random.fold_in(keys[6], part), 71), part),
        "self_mobility": jnp.clip(jnp.exp(math.log(1.6) - 1.3862944 * jax.random.uniform(own_keys[5], (N_ROW, GROUP_LEN), jnp.float32) ** block_scale(own_keys[5], (N_ROW, GROUP_LEN), ((0, 4),), -0.2, 0.2)), 0.4, 1.6),
    }


SHIFT = 1.0
HALF_WIDTH = 0.75


def apply_mobility(field_in, block_values, block_rows, block_cols, block_count, self_mobility):
    vectors = field_in.shape[0]
    span_len = 3 * CB
    grid_view = field_in.astype(jnp.float32).reshape(vectors, N_ROW, GB, span_len)
    tile_set = block_values.reshape(N_ROW * N_COL, SLOTS, span_len, span_len)
    row_ids = block_rows.reshape(N_ROW * N_COL, SLOTS).astype(jnp.int32)
    col_ids = block_cols.reshape(N_ROW * N_COL, SLOTS).astype(jnp.int32)
    live_counts = block_count.reshape(N_ROW * N_COL).astype(jnp.int32)
    owners = jnp.arange(N_ROW * N_COL, dtype=jnp.int32)
    slot_ids = jnp.arange(SLOTS, dtype=jnp.int32)
    self_grid = self_mobility.astype(jnp.float32).reshape(N_ROW, GB, span_len)

    def one_device(running, device_item):
        owner, tiles, rows_here, cols_here, live_count = device_item
        owner_row = owner // N_COL
        owner_col = owner % N_COL
        source = grid_view[:, owner_col]
        picked = source[:, cols_here]
        live_mask = (slot_ids < live_count).astype(jnp.float32)
        product = jnp.einsum("smk,vsk->vsm", tiles.astype(jnp.float32), picked) * live_mask[None, :, None]
        owner_part = jnp.zeros((vectors, GB, span_len), jnp.float32).at[:, rows_here].add(product)
        on_diagonal = (owner_row == owner_col).astype(jnp.float32)
        owner_part = owner_part + on_diagonal * (self_grid[owner_row] - SHIFT)[None] * source
        rounded = lax.optimization_barrier(owner_part.astype(jnp.bfloat16)).astype(jnp.float32)
        running = running.at[:, owner_row].add(rounded)
        return running, None

    start_sum = jnp.zeros((vectors, N_ROW, GB, span_len), jnp.float32)
    running = lax.scan(one_device, start_sum, (owners, tile_set, row_ids, col_ids, live_counts))[0]
    return running.reshape(vectors, N_ROW, GB * span_len)


def reference(noise, block_values, block_rows, block_cols, block_count, self_mobility):
    vectors = noise.shape[0]
    group_len = GB * 3 * CB
    piece_len = group_len // N_COL
    flat_noise = noise.reshape(vectors, N_ROW, group_len)
    first_sum = apply_mobility(flat_noise, block_values, block_rows, block_cols, block_count, self_mobility)
    first_term = (first_sum / HALF_WIDTH).astype(jnp.bfloat16)
    second_sum = apply_mobility(first_term, block_values, block_rows, block_cols, block_count, self_mobility)
    second_term = (2.0 * second_sum / HALF_WIDTH - flat_noise.astype(jnp.float32)).astype(jnp.bfloat16)
    return (first_term.reshape(vectors, N_COL, N_ROW, piece_len),
            second_term.reshape(vectors, N_ROW, N_COL, piece_len))
```

```python
import functools

import jax
import jax.numpy as jnp
from jax import lax
from jax.experimental import pallas as pl
from jax.experimental.pallas import tpu as pltpu
from jax.sharding import PartitionSpec as P

SHIFT = 1.0
HALF_WIDTH = 0.75

VMEM = pl.BlockSpec(memory_space=pltpu.VMEM)
SMEM = pl.BlockSpec(memory_space=pltpu.SMEM)


def pairing(size):
    if size & (size - 1) == 0:
        return (lambda i, k: i ^ k), (lambda i, k: i ^ k)
    return (lambda i, k: (i + k) % size), (lambda i, k: (i + size - k) % size)


def exchange(pieces, axis, size):
    to, _ = pairing(size)
    return [
        lax.ppermute(pieces[k - 1], axis, [(i, to(i, k)) for i in range(size)])
        for k in range(size - 1, 0, -1)
    ][::-1]


def lanes(start, length):
    return pl.ds(pl.multiple_of(start, 128), length)


def add_slots(source, total, tiles, read_at, write_at, live, contract):
    slots, span, _ = tiles.shape
    products = []
    for s in range(slots):
        picked = source[:, lanes(read_at[0, 0, s] * span, span)]
        products.append(
            lax.dot_general(
                picked, tiles[s], (((1,), (contract,)), ((), ())), preferred_element_type=jnp.float32
            )
        )
    for s in range(slots):
        at = lanes(write_at[0, 0, s] * span, span)
        total[:, at] += jnp.where(s < live, products[s], 0.0)


def self_factor():
    return (lax.axis_index("row") == lax.axis_index("col")).astype(jnp.float32)


def first_kernel(size, *refs):
    pieces, (tiles, rows, cols, count, self_mobility, out, whole, total) = refs[:size], refs[size:]
    _, source_of = pairing(size)
    me = lax.axis_index("col")
    piece = pieces[0].shape[1]
    for k in range(size):
        whole[:, lanes(source_of(me, k) * piece, piece)] = pieces[k][...]
    shift = self_factor() * (self_mobility[...] - SHIFT)
    total[...] = shift * whole[...].astype(jnp.float32)
    add_slots(whole, total, tiles, rows, cols, count[0, 0], 0)
    out[...] = total[...].astype(out.dtype)


def second_kernel(n_row, n_col, *refs):
    parts, (tiles, rows, cols, count, self_mobility), rest = (
        refs[:n_row],
        refs[n_row : n_row + 5],
        refs[n_row + 5 :],
    )
    first, outs, (whole, total) = rest[0], rest[1 : 1 + n_col], rest[1 + n_col :]
    sums = parts[0][...].astype(jnp.float32)
    for part in parts[1:]:
        sums = sums + part[...].astype(jnp.float32)
    whole[...] = (sums / HALF_WIDTH).astype(whole.dtype)
    row_piece = first.shape[1]
    first[...] = whole[:, lanes(lax.axis_index("row") * row_piece, row_piece)]
    shift = self_factor() * (self_mobility[...] - SHIFT)
    total[...] = shift * whole[...].astype(jnp.float32)
    add_slots(whole, total, tiles, cols, rows, count[0, 0], 1)
    to, _ = pairing(n_col)
    me = lax.axis_index("col")
    piece = outs[0].shape[1]
    for k in range(n_col):
        outs[k][...] = total[:, lanes(to(me, k) * piece, piece)].astype(outs[k].dtype)


def last_kernel(size, *refs):
    parts, (noise, out) = refs[:size], refs[size:]
    sums = parts[0][...].astype(jnp.float32)
    for part in parts[1:]:
        sums = sums + part[...].astype(jnp.float32)
    out[...] = (2.0 * sums / HALF_WIDTH - noise[...].astype(jnp.float32)).astype(out.dtype)


def on_device(noise, block_values, block_rows, block_cols, block_count, self_mobility):
    vectors, piece = noise.shape[0], noise.shape[3]
    n_row, n_col = lax.axis_size("row"), lax.axis_size("col")
    group_len = self_mobility.shape[1]
    own = noise.reshape(vectors, piece)
    tiles = block_values.reshape(block_values.shape[2:])
    whole_type = jax.ShapeDtypeStruct((vectors, group_len), jnp.bfloat16)
    piece_type = jax.ShapeDtypeStruct((vectors, piece), jnp.bfloat16)
    row_type = jax.ShapeDtypeStruct((vectors, group_len // n_row), jnp.bfloat16)
    table_specs = [VMEM, SMEM, SMEM, SMEM, VMEM]
    tables = (tiles, block_rows, block_cols, block_count, self_mobility)
    scratch = [
        pltpu.VMEM((vectors, group_len), jnp.bfloat16),
        pltpu.VMEM((vectors, group_len), jnp.float32),
    ]
    pieces = [own] + exchange([own] * (n_col - 1), "col", n_col)
    part = pl.pallas_call(
        functools.partial(first_kernel, n_col),
        out_shape=whole_type,
        in_specs=[VMEM] * n_col + table_specs,
        out_specs=VMEM,
        scratch_shapes=scratch,
        name="first_product",
    )(*pieces, *tables)
    parts = [part] + exchange([part] * (n_row - 1), "row", n_row)
    first, *seconds = pl.pallas_call(
        functools.partial(second_kernel, n_row, n_col),
        out_shape=[row_type] + [piece_type] * n_col,
        in_specs=[VMEM] * n_row + table_specs,
        out_specs=[VMEM] * (1 + n_col),
        scratch_shapes=scratch,
        name="second_product",
    )(*parts, *tables)
    arrived = [seconds[0]] + exchange(seconds[1:], "col", n_col)
    second = pl.pallas_call(
        functools.partial(last_kernel, n_col),
        out_shape=piece_type,
        in_specs=[VMEM] * (n_col + 1),
        out_specs=VMEM,
        name="second_term",
    )(*arrived, own)
    return first.reshape(vectors, 1, 1, -1), second.reshape(vectors, 1, 1, -1)


def solution(mesh):
    placed = (
        P("rep", "row", "col", None),
        P(("rep", "row"), "col", None, None, None),
        P(("rep", "row"), "col", None),
        P(("rep", "row"), "col", None),
        P(("rep", "row"), "col"),
        P(("rep", "row"), None),
    )
    return jax.shard_map(
        on_device,
        mesh=mesh,
        in_specs=placed,
        out_specs=(P("rep", "col", "row", None), P("rep", "row", "col", None)),
        check_vma=False,
    )
```

```python
import functools

import jax
import jax.numpy as jnp
from jax import lax
from jax.experimental import pallas as pl
from jax.experimental.pallas import tpu as pltpu
from jax.sharding import PartitionSpec as P

SHIFT = 1.0
HALF_WIDTH = 0.75
VMEM_LIMIT = 8 << 20
STAGE_LIMIT = 50 << 20

VMEM = pl.BlockSpec(memory_space=pltpu.VMEM)
HBM = pl.BlockSpec(memory_space=pltpu.HBM)
SMEM = pl.BlockSpec(memory_space=pltpu.SMEM)


def pairing(size):
    if size & (size - 1) == 0:
        return (lambda i, k: i ^ k), (lambda i, k: i ^ k)
    return (lambda i, k: (i + k) % size), (lambda i, k: (i + size - k) % size)


def exchange(pieces, axis, size):
    to, _ = pairing(size)
    return [
        lax.ppermute(pieces[k - 1], axis, [(i, to(i, k)) for i in range(size)])
        for k in range(size - 1, 0, -1)
    ][::-1]


def lanes(start, length):
    return pl.ds(pl.multiple_of(start, 128), length)


def add_slots(source, total, tiles, read_at, write_at, count, contract):
    slots, span, _ = tiles.shape
    live, spare = count[0, 0], source.shape[1] // span
    products = []
    for s in range(slots):
        picked = source[:, lanes(read_at[0, 0, s] * span, span)]
        products.append(
            lax.dot_general(
                picked, tiles[s], (((1,), (contract,)), ((), ())), preferred_element_type=jnp.float32
            )
        )
    for s in range(slots):
        at = lanes(jnp.where(s < live, write_at[0, 0, s], spare) * span, span)
        total[:, at] += products[s]


def self_factor():
    return (lax.axis_index("row") == lax.axis_index("col")).astype(jnp.float32)


def stage_kernel(values, tiles, sem):
    copy = pltpu.make_async_copy(values, tiles, sem)
    copy.start()
    copy.wait()


def first_kernel(size, *refs):
    pieces, (tiles, rows, cols, count, mobility, out, whole, total) = refs[:size], refs[size:]
    _, source_of = pairing(size)
    me = lax.axis_index("col")
    piece, group_len = pieces[0].shape[1], whole.shape[1]
    for k in range(size):
        whole[:, lanes(source_of(me, k) * piece, piece)] = pieces[k][...]
    total[:, :group_len] = self_factor() * (mobility[...] - SHIFT) * whole[...].astype(jnp.float32)
    add_slots(whole, total, tiles, rows, cols, count, 0)
    out[...] = total[:, :group_len].astype(out.dtype)


def second_kernel(n_row, n_col, *refs):
    parts, rest = refs[:n_row], refs[n_row + 5 :]
    tiles, rows, cols, count, mobility = refs[n_row : n_row + 5]
    first, outs, (whole, total) = rest[0], rest[1 : 1 + n_col], rest[1 + n_col :]
    group_len = whole.shape[1]
    sums = parts[0][...].astype(jnp.float32)
    for part in parts[1:]:
        sums = sums + part[...].astype(jnp.float32)
    whole[...] = (sums * (1.0 / HALF_WIDTH)).astype(whole.dtype)
    row_piece = first.shape[1]
    first[...] = whole[:, lanes(lax.axis_index("row") * row_piece, row_piece)]
    total[:, :group_len] = self_factor() * (mobility[...] - SHIFT) * whole[...].astype(jnp.float32)
    add_slots(whole, total, tiles, cols, rows, count, 1)
    to, _ = pairing(n_col)
    me = lax.axis_index("col")
    piece = outs[0].shape[1]
    for k in range(n_col):
        outs[k][...] = total[:, lanes(to(me, k) * piece, piece)].astype(outs[k].dtype)


def last_kernel(size, *refs):
    parts, (noise, out) = refs[:size], refs[size:]
    sums = parts[0][...].astype(jnp.float32)
    for part in parts[1:]:
        sums = sums + part[...].astype(jnp.float32)
    out[...] = ((2.0 / HALF_WIDTH) * sums - noise[...].astype(jnp.float32)).astype(out.dtype)


def on_device(noise, block_values, block_rows, block_cols, block_count, self_mobility):
    vectors, piece = noise.shape[0], noise.shape[3]
    n_row, n_col = lax.axis_size("row"), lax.axis_size("col")
    group_len = self_mobility.shape[1]
    own = noise.reshape(vectors, piece)
    tiles = block_values.reshape(block_values.shape[2:])
    whole_type = jax.ShapeDtypeStruct((vectors, group_len), jnp.bfloat16)
    piece_type = jax.ShapeDtypeStruct((vectors, piece), jnp.bfloat16)
    row_type = jax.ShapeDtypeStruct((vectors, group_len // n_row), jnp.bfloat16)
    span, slots = tiles.shape[-1], tiles.shape[0]
    scratch = [
        pltpu.VMEM((vectors, group_len), jnp.bfloat16),
        pltpu.VMEM((vectors, group_len + span), jnp.float32),
    ]
    params = pltpu.CompilerParams(vmem_limit_bytes=VMEM_LIMIT)
    arrived = exchange([own] * (n_col - 1), "col", n_col)
    staged = pl.pallas_call(
        stage_kernel,
        out_shape=jax.ShapeDtypeStruct(tiles.shape, tiles.dtype),
        in_specs=[HBM],
        out_specs=VMEM,
        scratch_shapes=[pltpu.SemaphoreType.DMA],
        compiler_params=pltpu.CompilerParams(vmem_limit_bytes=STAGE_LIMIT),
        cost_estimate=pl.CostEstimate(flops=0, transcendentals=0, bytes_accessed=4 * tiles.size),
        name="stage",
    )(tiles)
    tables = (staged, block_rows, block_cols, block_count, self_mobility)
    table_specs = [VMEM, SMEM, SMEM, SMEM, VMEM]
    pieces = [own] + arrived
    part = pl.pallas_call(
        functools.partial(first_kernel, n_col),
        out_shape=whole_type,
        in_specs=[VMEM] * n_col + table_specs,
        out_specs=VMEM,
        scratch_shapes=scratch,
        compiler_params=params,
        name="first_product",
    )(*pieces, *tables)
    parts = [part] + exchange([part] * (n_row - 1), "row", n_row)
    first, *seconds = pl.pallas_call(
        functools.partial(second_kernel, n_row, n_col),
        out_shape=[row_type] + [piece_type] * n_col,
        in_specs=[VMEM] * n_row + table_specs,
        out_specs=[VMEM] * (1 + n_col),
        scratch_shapes=scratch,
        compiler_params=params,
        name="second_product",
    )(*parts, *tables)
    arrived = [seconds[0]] + exchange(seconds[1:], "col", n_col)
    second = pl.pallas_call(
        functools.partial(last_kernel, n_col),
        out_shape=piece_type,
        in_specs=[VMEM] * (n_col + 1),
        out_specs=VMEM,
        compiler_params=params,
        name="second_term",
    )(*arrived, own)
    return first.reshape(vectors, 1, 1, -1), second.reshape(vectors, 1, 1, -1)


def solution(mesh):
    placed = (
        P("rep", "row", "col", None),
        P(("rep", "row"), "col", None, None, None),
        P(("rep", "row"), "col", None),
        P(("rep", "row"), "col", None),
        P(("rep", "row"), "col"),
        P(("rep", "row"), None),
    )
    return jax.shard_map(
        on_device,
        mesh=mesh,
        in_specs=placed,
        out_specs=(P("rep", "col", "row", None), P("rep", "row", "col", None)),
        check_vma=False,
    )
```

```python
import functools

import jax
import jax.numpy as jnp
from jax import lax
from jax.experimental import pallas as pl
from jax.experimental.pallas import tpu as pltpu
from jax.sharding import PartitionSpec as P

SHIFT = 1.0
HALF_WIDTH = 0.75
VMEM_LIMIT = 8 << 20
STAGE_LIMIT = 50 << 20

VMEM = pl.BlockSpec(memory_space=pltpu.VMEM)
HBM = pl.BlockSpec(memory_space=pltpu.HBM)
SMEM = pl.BlockSpec(memory_space=pltpu.SMEM)


def pairing(size):
    if size & (size - 1) == 0:
        return (lambda i, k: i ^ k), (lambda i, k: i ^ k)
    return (lambda i, k: (i + k) % size), (lambda i, k: (i + size - k) % size)


def exchange(pieces, axis, size):
    to, _ = pairing(size)
    return [
        lax.ppermute(pieces[k - 1], axis, [(i, to(i, k)) for i in range(size)])
        for k in range(size - 1, 0, -1)
    ][::-1]


def gather_pairs(part, axis, size):
    if size & (size - 1):
        return exchange([part] * (size - 1), axis, size)
    swap = [(i, i ^ 1) for i in range(size)]
    far = [lax.ppermute(part, axis, [(i, i ^ k) for i in range(size)]) for k in range(2, size, 2)]
    near = [lax.ppermute(a, axis, swap) for a in [part] + far]
    return near + far


def lanes(start, length):
    return pl.ds(pl.multiple_of(start, 128), length)


def add_slots(source, total, tiles, read_at, write_at, count, contract):
    slots, span, _ = tiles.shape
    live, spare = count[0, 0], source.shape[1] // span
    products = []
    for s in range(slots):
        picked = source[:, lanes(read_at[0, 0, s] * span, span)]
        products.append(
            lax.dot_general(
                picked, tiles[s], (((1,), (contract,)), ((), ())), preferred_element_type=jnp.float32
            )
        )
    for s in range(slots):
        at = lanes(jnp.where(s < live, write_at[0, 0, s], spare) * span, span)
        total[:, at] += products[s]


def self_factor():
    return (lax.axis_index("row") == lax.axis_index("col")).astype(jnp.float32)


def stage_kernel(values, tiles, sem):
    copy = pltpu.make_async_copy(values, tiles, sem)
    copy.start()
    copy.wait()


def first_kernel(size, *refs):
    pieces, (tiles, rows, cols, count, mobility, out, whole, total) = refs[:size], refs[size:]
    _, source_of = pairing(size)
    me = lax.axis_index("col")
    piece, group_len = pieces[0].shape[1], whole.shape[1]
    for k in range(size):
        whole[:, lanes(source_of(me, k) * piece, piece)] = pieces[k][...]
    total[:, :group_len] = self_factor() * (mobility[...] - SHIFT) * whole[...].astype(jnp.float32)
    add_slots(whole, total, tiles, rows, cols, count, 0)
    out[...] = total[:, :group_len].astype(out.dtype)


def second_kernel(n_row, n_col, *refs):
    parts, rest = refs[:n_row], refs[n_row + 5 :]
    tiles, rows, cols, count, mobility = refs[n_row : n_row + 5]
    first, outs, (whole, total) = rest[0], rest[1 : 1 + n_col], rest[1 + n_col :]
    group_len = whole.shape[1]
    sums = parts[0][...].astype(jnp.float32)
    for part in parts[1:]:
        sums = sums + part[...].astype(jnp.float32)
    whole[...] = (sums * (1.0 / HALF_WIDTH)).astype(whole.dtype)
    row_piece = first.shape[1]
    first[...] = whole[:, lanes(lax.axis_index("row") * row_piece, row_piece)]
    total[:, :group_len] = self_factor() * (mobility[...] - SHIFT) * whole[...].astype(jnp.float32)
    add_slots(whole, total, tiles, cols, rows, count, 1)
    to, _ = pairing(n_col)
    me = lax.axis_index("col")
    piece = outs[0].shape[1]
    for k in range(n_col):
        outs[k][...] = total[:, lanes(to(me, k) * piece, piece)].astype(outs[k].dtype)


def last_kernel(size, *refs):
    parts, (noise, first, first_out, out) = refs[:size], refs[size:]
    first_out[...] = first[...]
    sums = parts[0][...].astype(jnp.float32)
    for part in parts[1:]:
        sums = sums + part[...].astype(jnp.float32)
    out[...] = ((2.0 / HALF_WIDTH) * sums - noise[...].astype(jnp.float32)).astype(out.dtype)


def on_device(noise, block_values, block_rows, block_cols, block_count, self_mobility):
    vectors, piece = noise.shape[0], noise.shape[3]
    n_row, n_col = lax.axis_size("row"), lax.axis_size("col")
    group_len = self_mobility.shape[1]
    own = noise.reshape(vectors, piece)
    tiles = block_values.reshape(block_values.shape[2:])
    whole_type = jax.ShapeDtypeStruct((vectors, group_len), jnp.bfloat16)
    piece_type = jax.ShapeDtypeStruct((vectors, piece), jnp.bfloat16)
    row_type = jax.ShapeDtypeStruct((vectors, group_len // n_row), jnp.bfloat16)
    span, slots = tiles.shape[-1], tiles.shape[0]
    scratch = [
        pltpu.VMEM((vectors, group_len), jnp.bfloat16),
        pltpu.VMEM((vectors, group_len + span), jnp.float32),
    ]
    params = pltpu.CompilerParams(vmem_limit_bytes=VMEM_LIMIT)
    arrived = exchange([own] * (n_col - 1), "col", n_col)
    staged = pl.pallas_call(
        stage_kernel,
        out_shape=jax.ShapeDtypeStruct(tiles.shape, tiles.dtype),
        in_specs=[HBM],
        out_specs=VMEM,
        scratch_shapes=[pltpu.SemaphoreType.DMA],
        compiler_params=pltpu.CompilerParams(vmem_limit_bytes=STAGE_LIMIT),
        cost_estimate=pl.CostEstimate(flops=0, transcendentals=0, bytes_accessed=4 * tiles.size),
        name="stage",
    )(tiles)
    tables = (staged, block_rows, block_cols, block_count, self_mobility)
    table_specs = [VMEM, SMEM, SMEM, SMEM, VMEM]
    pieces = [own] + arrived
    part = pl.pallas_call(
        functools.partial(first_kernel, n_col),
        out_shape=whole_type,
        in_specs=[VMEM] * n_col + table_specs,
        out_specs=VMEM,
        scratch_shapes=scratch,
        compiler_params=params,
        name="first_product",
    )(*pieces, *tables)
    parts = [part] + gather_pairs(part, "row", n_row)
    first, *seconds = pl.pallas_call(
        functools.partial(second_kernel, n_row, n_col),
        out_shape=[row_type] + [piece_type] * n_col,
        in_specs=[VMEM] * n_row + table_specs,
        out_specs=[VMEM] * (1 + n_col),
        scratch_shapes=scratch,
        compiler_params=params,
        name="second_product",
    )(*parts, *tables)
    arrived = [seconds[0]] + exchange(seconds[1:], "col", n_col)
    first, second = pl.pallas_call(
        functools.partial(last_kernel, n_col),
        out_shape=[row_type, piece_type],
        in_specs=[VMEM] * (n_col + 2),
        out_specs=[VMEM] * 2,
        compiler_params=params,
        name="second_term",
    )(*arrived[::-1], own, first)
    return first.reshape(vectors, 1, 1, -1), second.reshape(vectors, 1, 1, -1)


def solution(mesh):
    placed = (
        P("rep", "row", "col", None),
        P(("rep", "row"), "col", None, None, None),
        P(("rep", "row"), "col", None),
        P(("rep", "row"), "col", None),
        P(("rep", "row"), "col"),
        P(("rep", "row"), None),
    )
    return jax.shard_map(
        on_device,
        mesh=mesh,
        in_specs=placed,
        out_specs=(P("rep", "col", "row", None), P("rep", "row", "col", None)),
        check_vma=False,
    )
```

```python
import functools

import jax
import jax.numpy as jnp
from jax import lax
from jax.experimental import pallas as pl
from jax.experimental.pallas import tpu as pltpu
from jax.sharding import PartitionSpec as P

SHIFT = 1.0
HALF_WIDTH = 0.75
VMEM_LIMIT = 8 << 20
STAGE_LIMIT = 50 << 20

VMEM = pl.BlockSpec(memory_space=pltpu.VMEM)
HBM = pl.BlockSpec(memory_space=pltpu.HBM)


def pairing(size):
    if size & (size - 1) == 0:
        return (lambda i, k: i ^ k), (lambda i, k: i ^ k)
    return (lambda i, k: (i + k) % size), (lambda i, k: (i + size - k) % size)


def exchange(pieces, axis, size):
    to, _ = pairing(size)
    return [
        lax.ppermute(pieces[k - 1], axis, [(i, to(i, k)) for i in range(size)])
        for k in range(size - 1, 0, -1)
    ][::-1]


def gather_pairs(part, axis, size):
    if size & (size - 1):
        return exchange([part] * (size - 1), axis, size)
    swap = [(i, i ^ 1) for i in range(size)]
    far = [lax.ppermute(part, axis, [(i, i ^ k) for i in range(size)]) for k in range(2, size, 2)]
    near = [lax.ppermute(a, axis, swap) for a in [part] + far]
    return near + far


def lanes(start, length):
    return pl.ds(pl.multiple_of(start, 128), length)


def add_slots(source, total, tiles, read_at, write_at, count):
    slots, span, _ = tiles.shape
    live, spare = count[...][0, 0], source.shape[1] // span
    read_at, write_at = read_at[...], write_at[...]
    products = []
    for s in range(slots):
        picked = source[:, lanes(read_at[0, 0, s] * span, span)]
        products.append(jnp.dot(picked, tiles[s], preferred_element_type=jnp.float32))
    for s in range(slots):
        at = lanes(jnp.where(s < live, write_at[0, 0, s], spare) * span, span)
        total[:, at] += products[s]


def self_factor():
    return (lax.axis_index("row") == lax.axis_index("col")).astype(jnp.float32)


def stage_kernel(values, tiles, sem):
    copy = pltpu.make_async_copy(values, tiles, sem)
    copy.start()
    copy.wait()


def turn_kernel(tiles, turned):
    for s in range(tiles.shape[0]):
        turned[s] = tiles[s].T


def first_kernel(size, *refs):
    pieces, (tiles, rows, cols, count, mobility, out, whole, total) = refs[:size], refs[size:]
    _, source_of = pairing(size)
    me = lax.axis_index("col")
    piece, group_len = pieces[0].shape[1], whole.shape[1]
    for k in range(size):
        whole[:, lanes(source_of(me, k) * piece, piece)] = pieces[k][...]
    total[:, :group_len] = self_factor() * (mobility[...] - SHIFT) * whole[...].astype(jnp.float32)
    add_slots(whole, total, tiles, rows, cols, count)
    out[...] = total[:, :group_len].astype(out.dtype)


def second_kernel(n_row, n_col, *refs):
    parts, rest = refs[:n_row], refs[n_row + 5 :]
    tiles, rows, cols, count, mobility = refs[n_row : n_row + 5]
    first, outs, (whole, total) = rest[0], rest[1 : 1 + n_col], rest[1 + n_col :]
    group_len = whole.shape[1]
    sums = parts[0][...].astype(jnp.float32)
    for part in parts[1:]:
        sums = sums + part[...].astype(jnp.float32)
    whole[...] = (sums * (1.0 / HALF_WIDTH)).astype(whole.dtype)
    row_piece = first.shape[1]
    first[...] = whole[:, lanes(lax.axis_index("row") * row_piece, row_piece)]
    total[:, :group_len] = self_factor() * (mobility[...] - SHIFT) * whole[...].astype(jnp.float32)
    add_slots(whole, total, tiles, cols, rows, count)
    to, _ = pairing(n_col)
    me = lax.axis_index("col")
    piece = outs[0].shape[1]
    for k in range(n_col):
        outs[k][...] = total[:, lanes(to(me, k) * piece, piece)].astype(outs[k].dtype)


def last_kernel(size, *refs):
    parts, (noise, first, first_out, out) = refs[:size], refs[size:]
    first_out[...] = first[...]
    sums = parts[0][...].astype(jnp.float32)
    for part in parts[1:]:
        sums = sums + part[...].astype(jnp.float32)
    out[...] = ((2.0 / HALF_WIDTH) * sums - noise[...].astype(jnp.float32)).astype(out.dtype)


def on_device(noise, block_values, block_rows, block_cols, block_count, self_mobility):
    vectors, piece = noise.shape[0], noise.shape[3]
    n_row, n_col = lax.axis_size("row"), lax.axis_size("col")
    group_len = self_mobility.shape[1]
    own = noise.reshape(vectors, piece)
    tiles = block_values.reshape(block_values.shape[2:])
    whole_type = jax.ShapeDtypeStruct((vectors, group_len), jnp.bfloat16)
    piece_type = jax.ShapeDtypeStruct((vectors, piece), jnp.bfloat16)
    row_type = jax.ShapeDtypeStruct((vectors, group_len // n_row), jnp.bfloat16)
    span, slots = tiles.shape[-1], tiles.shape[0]
    scratch = [
        pltpu.VMEM((vectors, group_len), jnp.bfloat16),
        pltpu.VMEM((vectors, group_len + span), jnp.float32),
    ]
    params = pltpu.CompilerParams(vmem_limit_bytes=VMEM_LIMIT)
    arrived = exchange([own] * (n_col - 1), "col", n_col)
    staged = pl.pallas_call(
        stage_kernel,
        out_shape=jax.ShapeDtypeStruct(tiles.shape, tiles.dtype),
        in_specs=[HBM],
        out_specs=VMEM,
        scratch_shapes=[pltpu.SemaphoreType.DMA],
        compiler_params=pltpu.CompilerParams(vmem_limit_bytes=STAGE_LIMIT),
        cost_estimate=pl.CostEstimate(flops=0, transcendentals=0, bytes_accessed=4 * tiles.size),
        name="stage",
    )(tiles)
    turned = pl.pallas_call(
        turn_kernel,
        out_shape=jax.ShapeDtypeStruct(tiles.shape, tiles.dtype),
        in_specs=[VMEM],
        out_specs=VMEM,
        compiler_params=params,
        cost_estimate=pl.CostEstimate(flops=0, transcendentals=0, bytes_accessed=4 * tiles.size),
        name="turn",
    )(staged)
    tables = (staged, block_rows, block_cols, block_count, self_mobility)
    table_specs = [VMEM, VMEM, VMEM, VMEM, VMEM]
    pieces = [own] + arrived
    part = pl.pallas_call(
        functools.partial(first_kernel, n_col),
        out_shape=whole_type,
        in_specs=[VMEM] * n_col + table_specs,
        out_specs=VMEM,
        scratch_shapes=scratch,
        compiler_params=params,
        name="first_product",
    )(*pieces, *tables)
    parts = [part] + gather_pairs(part, "row", n_row)
    first, *seconds = pl.pallas_call(
        functools.partial(second_kernel, n_row, n_col),
        out_shape=[row_type] + [piece_type] * n_col,
        in_specs=[VMEM] * n_row + table_specs,
        out_specs=[VMEM] * (1 + n_col),
        scratch_shapes=scratch,
        compiler_params=params,
        name="second_product",
    )(*parts, turned, *tables[1:])
    arrived = [seconds[0]] + exchange(seconds[1:], "col", n_col)
    first, second = pl.pallas_call(
        functools.partial(last_kernel, n_col),
        out_shape=[row_type, piece_type],
        in_specs=[VMEM] * (n_col + 2),
        out_specs=[VMEM] * 2,
        compiler_params=params,
        name="second_term",
    )(*arrived[::-1], own, first)
    return first.reshape(vectors, 1, 1, -1), second.reshape(vectors, 1, 1, -1)


def solution(mesh):
    placed = (
        P("rep", "row", "col", None),
        P(("rep", "row"), "col", None, None, None),
        P(("rep", "row"), "col", None),
        P(("rep", "row"), "col", None),
        P(("rep", "row"), "col"),
        P(("rep", "row"), None),
    )
    return jax.shard_map(
        on_device,
        mesh=mesh,
        in_specs=placed,
        out_specs=(P("rep", "col", "row", None), P("rep", "row", "col", None)),
        check_vma=False,
    )
```

```python
import functools

import jax
import jax.numpy as jnp
from jax import lax
from jax.experimental import pallas as pl
from jax.experimental.pallas import tpu as pltpu
from jax.sharding import PartitionSpec as P

SHIFT = 1.0
HALF_WIDTH = 0.75
VMEM_LIMIT = 8 << 20
STAGE_LIMIT = 50 << 20

VMEM = pl.BlockSpec(memory_space=pltpu.VMEM)
HBM = pl.BlockSpec(memory_space=pltpu.HBM)


def offsets(size):
    if size & (size - 1):
        return [[(i + k) % size for i in range(size)] for k in range(1, size)]
    return [[i ^ k for i in range(size)] for k in range(1, size)]


def rounds(size):
    if size == 4:
        return [[2, 0, 3, 1], [3, 2, 1, 0], [1, 3, 0, 2]]
    return offsets(size)


def pick(table, at):
    value = table[0]
    for i in range(1, len(table)):
        value = jnp.where(at == i, table[i], value)
    return value


def send(pieces, axis, permutations):
    return [
        lax.ppermute(piece, axis, list(enumerate(target)))
        for piece, target in zip(pieces, permutations)
    ]


def gather_pairs(part, axis, size):
    if size & (size - 1):
        return send([part] * (size - 1), axis, offsets(size))
    swap = [(i, i ^ 1) for i in range(size)]
    far = [lax.ppermute(part, axis, [(i, i ^ k) for i in range(size)]) for k in range(2, size, 2)]
    near = [lax.ppermute(a, axis, swap) for a in [part] + far]
    return near + far


def lanes(start, length):
    return pl.ds(pl.multiple_of(start, 128), length)


def add_slots(source, total, tiles, read_at, write_at, count):
    slots, span, _ = tiles.shape
    live, spare = count[...][0, 0], source.shape[1] // span
    read_at, write_at = read_at[...], write_at[...]
    products = []
    for s in range(slots):
        picked = source[:, lanes(read_at[0, 0, s] * span, span)]
        products.append(jnp.dot(picked, tiles[s], preferred_element_type=jnp.float32))
    for s in range(slots):
        at = lanes(jnp.where(s < live, write_at[0, 0, s], spare) * span, span)
        total[:, at] += products[s]


def self_factor():
    return (lax.axis_index("row") == lax.axis_index("col")).astype(jnp.float32)


def stage_kernel(values, tiles, sems):
    copies = [
        pltpu.make_async_copy(values.at[s], tiles.at[s], sems.at[s]) for s in range(tiles.shape[0])
    ]
    for copy in copies:
        copy.start()
    for copy in copies:
        copy.wait()


def turn_kernel(tiles, turned):
    for s in range(tiles.shape[0]):
        turned[s] = tiles[s].T


def first_kernel(size, *refs):
    pieces, (tiles, rows, cols, count, mobility, out, whole, total) = refs[:size], refs[size:]
    me = lax.axis_index("col")
    piece, group_len = pieces[0].shape[1], whole.shape[1]
    sources = [me] + [pick([target.index(i) for i in range(size)], me) for target in rounds(size)]
    for source, arrived in zip(sources, pieces):
        whole[:, lanes(source * piece, piece)] = arrived[...]
    total[:, :group_len] = self_factor() * (mobility[...] - SHIFT) * whole[...].astype(jnp.float32)
    add_slots(whole, total, tiles, rows, cols, count)
    out[...] = total[:, :group_len].astype(out.dtype)


def second_kernel(n_row, n_col, *refs):
    parts, rest = refs[:n_row], refs[n_row + 5 :]
    tiles, rows, cols, count, mobility = refs[n_row : n_row + 5]
    first, outs, (whole, total) = rest[0], rest[1 : 1 + n_col], rest[1 + n_col :]
    group_len = whole.shape[1]
    sums = parts[0][...].astype(jnp.float32)
    for part in parts[1:]:
        sums = sums + part[...].astype(jnp.float32)
    whole[...] = (sums * (1.0 / HALF_WIDTH)).astype(whole.dtype)
    row_piece = first.shape[1]
    first[...] = whole[:, lanes(lax.axis_index("row") * row_piece, row_piece)]
    total[:, :group_len] = self_factor() * (mobility[...] - SHIFT) * whole[...].astype(jnp.float32)
    add_slots(whole, total, tiles, cols, rows, count)
    me = lax.axis_index("col")
    piece = outs[0].shape[1]
    for target, out in zip([me] + [pick(p, me) for p in offsets(n_col)], outs):
        out[...] = total[:, lanes(target * piece, piece)].astype(out.dtype)


def last_kernel(size, *refs):
    parts, (noise, first, first_out, out) = refs[:size], refs[size:]
    first_out[...] = first[...]
    sums = parts[0][...].astype(jnp.float32)
    for part in parts[1:]:
        sums = sums + part[...].astype(jnp.float32)
    out[...] = ((2.0 / HALF_WIDTH) * sums - noise[...].astype(jnp.float32)).astype(out.dtype)


def on_device(noise, block_values, block_rows, block_cols, block_count, self_mobility):
    vectors, piece = noise.shape[0], noise.shape[3]
    n_row, n_col = lax.axis_size("row"), lax.axis_size("col")
    group_len = self_mobility.shape[1]
    own = noise.reshape(vectors, piece)
    tiles = block_values.reshape(block_values.shape[2:])
    whole_type = jax.ShapeDtypeStruct((vectors, group_len), jnp.bfloat16)
    piece_type = jax.ShapeDtypeStruct((vectors, piece), jnp.bfloat16)
    row_type = jax.ShapeDtypeStruct((vectors, group_len // n_row), jnp.bfloat16)
    span, slots = tiles.shape[-1], tiles.shape[0]
    scratch = [
        pltpu.VMEM((vectors, group_len), jnp.bfloat16),
        pltpu.VMEM((vectors, group_len + span), jnp.float32),
    ]
    params = pltpu.CompilerParams(vmem_limit_bytes=VMEM_LIMIT)
    arrived = send([own] * (n_col - 1), "col", rounds(n_col))
    staged = pl.pallas_call(
        stage_kernel,
        out_shape=jax.ShapeDtypeStruct(tiles.shape, tiles.dtype),
        in_specs=[HBM],
        out_specs=VMEM,
        scratch_shapes=[pltpu.SemaphoreType.DMA((slots,))],
        compiler_params=pltpu.CompilerParams(vmem_limit_bytes=STAGE_LIMIT),
        cost_estimate=pl.CostEstimate(flops=0, transcendentals=0, bytes_accessed=4 * tiles.size),
        name="stage",
    )(tiles)
    turned = pl.pallas_call(
        turn_kernel,
        out_shape=jax.ShapeDtypeStruct(tiles.shape, tiles.dtype),
        in_specs=[VMEM],
        out_specs=VMEM,
        compiler_params=params,
        cost_estimate=pl.CostEstimate(flops=0, transcendentals=0, bytes_accessed=4 * tiles.size),
        name="turn",
    )(staged)
    tables = (staged, block_rows, block_cols, block_count, self_mobility)
    table_specs = [VMEM, VMEM, VMEM, VMEM, VMEM]
    pieces = [own] + arrived
    part = pl.pallas_call(
        functools.partial(first_kernel, n_col),
        out_shape=whole_type,
        in_specs=[VMEM] * n_col + table_specs,
        out_specs=VMEM,
        scratch_shapes=scratch,
        compiler_params=params,
        name="first_product",
    )(*pieces, *tables)
    parts = [part] + gather_pairs(part, "row", n_row)
    first, *seconds = pl.pallas_call(
        functools.partial(second_kernel, n_row, n_col),
        out_shape=[row_type] + [piece_type] * n_col,
        in_specs=[VMEM] * n_row + table_specs,
        out_specs=[VMEM] * (1 + n_col),
        scratch_shapes=scratch,
        compiler_params=params,
        name="second_product",
    )(*parts, turned, *tables[1:])
    arrived = [seconds[0]] + send(seconds[1:], "col", offsets(n_col))
    first, second = pl.pallas_call(
        functools.partial(last_kernel, n_col),
        out_shape=[row_type, piece_type],
        in_specs=[VMEM] * (n_col + 2),
        out_specs=[VMEM] * 2,
        compiler_params=params,
        name="second_term",
    )(*arrived[::-1], own, first)
    return first.reshape(vectors, 1, 1, -1), second.reshape(vectors, 1, 1, -1)


def solution(mesh):
    placed = (
        P("rep", "row", "col", None),
        P(("rep", "row"), "col", None, None, None),
        P(("rep", "row"), "col", None),
        P(("rep", "row"), "col", None),
        P(("rep", "row"), "col"),
        P(("rep", "row"), None),
    )
    return jax.shard_map(
        on_device,
        mesh=mesh,
        in_specs=placed,
        out_specs=(P("rep", "col", "row", None), P("rep", "row", "col", None)),
        check_vma=False,
    )
```

```python
import functools

import jax
import jax.numpy as jnp
from jax import lax
from jax.experimental import pallas as pl
from jax.experimental.pallas import tpu as pltpu
from jax.sharding import PartitionSpec as P

SHIFT = 1.0
HALF_WIDTH = 0.75
VMEM_LIMIT = 8 << 20
STAGE_LIMIT = 50 << 20

VMEM = pl.BlockSpec(memory_space=pltpu.VMEM)
HBM = pl.BlockSpec(memory_space=pltpu.HBM)


def offsets(size):
    if size & (size - 1):
        return [[(i + k) % size for i in range(size)] for k in range(1, size)]
    return [[i ^ k for i in range(size)] for k in range(1, size)]


def rounds(size):
    if size == 4:
        return [[1, 3, 0, 2], [3, 2, 1, 0], [2, 0, 3, 1]]
    return offsets(size)


def pick(table, at):
    value = table[0]
    for i in range(1, len(table)):
        value = jnp.where(at == i, table[i], value)
    return value


def send(pieces, axis, permutations):
    return [
        lax.ppermute(piece, axis, list(enumerate(target)))
        for piece, target in zip(pieces, permutations)
    ]


def gather_pairs(part, axis, size):
    if size & (size - 1):
        return [part], send([part] * (size - 1), axis, offsets(size))
    swap = [(i, i ^ 1) for i in range(size)]
    far = [lax.ppermute(part, axis, [(i, i ^ k) for i in range(size)]) for k in range(2, size, 2)]
    near = [lax.ppermute(a, axis, swap) for a in [part] + far]
    return [part, near[0], *far], near[1:]


def lanes(start, length):
    return pl.ds(pl.multiple_of(start, 128), length)


def add_slots(source, total, tiles, read_at, write_at, count):
    slots, span, _ = tiles.shape
    live, spare = count[...][0, 0], source.shape[1] // span
    read_at, write_at = read_at[...], write_at[...]
    products = []
    for s in range(slots):
        picked = source[:, lanes(read_at[0, 0, s] * span, span)]
        products.append(jnp.dot(picked, tiles[s], preferred_element_type=jnp.float32))
    for s in range(slots):
        at = lanes(jnp.where(s < live, write_at[0, 0, s], spare) * span, span)
        total[:, at] += products[s]


def self_factor():
    return (lax.axis_index("row") == lax.axis_index("col")).astype(jnp.float32)


def stage_kernel(values, tiles, sems):
    copies = [
        pltpu.make_async_copy(values.at[s], tiles.at[s], sems.at[s]) for s in range(tiles.shape[0])
    ]
    for copy in copies:
        copy.start()
    for copy in copies:
        copy.wait()


def added(parts):
    sums = parts[0][...].astype(jnp.float32)
    for part in parts[1:]:
        sums = sums + part[...].astype(jnp.float32)
    return sums


def turn_kernel(tiles, *refs):
    parts, (turned, sums) = refs[:-2], refs[-2:]
    sums[...] = added(parts)
    for s in range(tiles.shape[0]):
        turned[s] = tiles[s].T


def first_kernel(size, *refs):
    pieces, (tiles, rows, cols, count, mobility, out, whole, total) = refs[:size], refs[size:]
    me = lax.axis_index("col")
    piece, group_len = pieces[0].shape[1], whole.shape[1]
    sources = [me] + [pick([target.index(i) for i in range(size)], me) for target in rounds(size)]
    for source, arrived in zip(sources, pieces):
        whole[:, lanes(source * piece, piece)] = arrived[...]
    total[:, :group_len] = self_factor() * (mobility[...] - SHIFT) * whole[...].astype(jnp.float32)
    add_slots(whole, total, tiles, rows, cols, count)
    out[...] = total[:, :group_len].astype(out.dtype)


def second_kernel(n_parts, n_col, *refs):
    parts, rest = refs[:n_parts], refs[n_parts + 5 :]
    tiles, rows, cols, count, mobility = refs[n_parts : n_parts + 5]
    first, outs, (whole, total) = rest[0], rest[1 : 1 + n_col], rest[1 + n_col :]
    group_len = whole.shape[1]
    whole[...] = (added(parts) * (1.0 / HALF_WIDTH)).astype(whole.dtype)
    row_piece = first.shape[1]
    first[...] = whole[:, lanes(lax.axis_index("row") * row_piece, row_piece)]
    total[:, :group_len] = self_factor() * (mobility[...] - SHIFT) * whole[...].astype(jnp.float32)
    add_slots(whole, total, tiles, cols, rows, count)
    me = lax.axis_index("col")
    piece = outs[0].shape[1]
    for target, out in zip([me] + [pick(p, me) for p in offsets(n_col)], outs):
        out[...] = total[:, lanes(target * piece, piece)].astype(out.dtype)


def last_kernel(size, *refs):
    parts, (noise, first, first_out, out) = refs[:size], refs[size:]
    first_out[...] = first[...]
    out[...] = ((2.0 / HALF_WIDTH) * added(parts) - noise[...].astype(jnp.float32)).astype(out.dtype)


def on_device(noise, block_values, block_rows, block_cols, block_count, self_mobility):
    vectors, piece = noise.shape[0], noise.shape[3]
    n_row, n_col = lax.axis_size("row"), lax.axis_size("col")
    group_len = self_mobility.shape[1]
    own = noise.reshape(vectors, piece)
    tiles = block_values.reshape(block_values.shape[2:])
    whole_type = jax.ShapeDtypeStruct((vectors, group_len), jnp.bfloat16)
    piece_type = jax.ShapeDtypeStruct((vectors, piece), jnp.bfloat16)
    row_type = jax.ShapeDtypeStruct((vectors, group_len // n_row), jnp.bfloat16)
    span, slots = tiles.shape[-1], tiles.shape[0]
    scratch = [
        pltpu.VMEM((vectors, group_len), jnp.bfloat16),
        pltpu.VMEM((vectors, group_len + span), jnp.float32),
    ]
    params = pltpu.CompilerParams(vmem_limit_bytes=VMEM_LIMIT)
    arrived = send([own] * (n_col - 1), "col", rounds(n_col))
    staged = pl.pallas_call(
        stage_kernel,
        out_shape=jax.ShapeDtypeStruct(tiles.shape, tiles.dtype),
        in_specs=[HBM],
        out_specs=VMEM,
        scratch_shapes=[pltpu.SemaphoreType.DMA((slots,))],
        compiler_params=pltpu.CompilerParams(vmem_limit_bytes=STAGE_LIMIT),
        cost_estimate=pl.CostEstimate(flops=0, transcendentals=0, bytes_accessed=4 * tiles.size),
        name="stage",
    )(tiles)
    tables = (staged, block_rows, block_cols, block_count, self_mobility)
    table_specs = [VMEM, VMEM, VMEM, VMEM, VMEM]
    pieces = [own] + arrived
    part = pl.pallas_call(
        functools.partial(first_kernel, n_col),
        out_shape=whole_type,
        in_specs=[VMEM] * n_col + table_specs,
        out_specs=VMEM,
        scratch_shapes=scratch,
        compiler_params=params,
        name="first_product",
    )(*pieces, *tables)
    here, late = gather_pairs(part, "row", n_row)
    turned, summed = pl.pallas_call(
        turn_kernel,
        out_shape=[
            jax.ShapeDtypeStruct(tiles.shape, tiles.dtype),
            jax.ShapeDtypeStruct((vectors, group_len), jnp.float32),
        ],
        in_specs=[VMEM] * (1 + len(here)),
        out_specs=[VMEM] * 2,
        compiler_params=params,
        cost_estimate=pl.CostEstimate(flops=0, transcendentals=0, bytes_accessed=4 * tiles.size),
        name="turn",
    )(staged, *here)
    parts = [summed, *late]
    first, *seconds = pl.pallas_call(
        functools.partial(second_kernel, len(parts), n_col),
        out_shape=[row_type] + [piece_type] * n_col,
        in_specs=[VMEM] * len(parts) + table_specs,
        out_specs=[VMEM] * (1 + n_col),
        scratch_shapes=scratch,
        compiler_params=params,
        name="second_product",
    )(*parts, turned, *tables[1:])
    arrived = [seconds[0]] + send(seconds[1:], "col", offsets(n_col))
    first, second = pl.pallas_call(
        functools.partial(last_kernel, n_col),
        out_shape=[row_type, piece_type],
        in_specs=[VMEM] * (n_col + 2),
        out_specs=[VMEM] * 2,
        compiler_params=params,
        name="second_term",
    )(*arrived[::-1], own, first)
    return first.reshape(vectors, 1, 1, -1), second.reshape(vectors, 1, 1, -1)


def solution(mesh):
    placed = (
        P("rep", "row", "col", None),
        P(("rep", "row"), "col", None, None, None),
        P(("rep", "row"), "col", None),
        P(("rep", "row"), "col", None),
        P(("rep", "row"), "col"),
        P(("rep", "row"), None),
    )
    return jax.shard_map(
        on_device,
        mesh=mesh,
        in_specs=placed,
        out_specs=(P("rep", "col", "row", None), P("rep", "row", "col", None)),
        check_vma=False,
    )
```
